256 devices in a mesh: tm: 32 (over z, x_hi, core), chan: 4 (over y), row: 2 (over x_lo).
Axes of the slice: x: 4 (x_hi: 2, x_lo: 2; x = x_hi * 2 + x_lo), y: 4, z: 8, core: 2. Of those that a mesh axis runs over, the one named last changes fastest.
Arguments:
- video: bfloat16 [128, 68, 32, 512], P('tm', 'row', None, 'chan'), may hold values from -6 to 6
- depthwise_kernel: float32 [3, 3, 512], P(None, None, 'chan'), may hold values from -2 to 2
- down_weight: bfloat16 [3, 512, 512], P(None, None, 'chan'), may hold values from -0.15625 to 0.15625
- up_weight: bfloat16 [3, 512, 512], P(None, None, 'chan'), may hold values from -0.1875 to 0.1875
- cotangent: bfloat16 [128, 68, 32, 512], P('tm', 'row', None, 'chan'), may hold values from -6 to 6
Outputs:
- result: bfloat16 [128, 68, 32, 512], P('tm', 'row', None, 'chan')
- grad_video: bfloat16 [128, 68, 32, 512], P('tm', 'row', None, 'chan')
- depthwise_kernel_gradient: float32 [3, 3, 512], P(None, None, 'chan')
- grad_down: float32 [3, 512, 512], P(None, None, 'chan')
- grad_up: float32 [3, 512, 512], P(None, None, 'chan')
The draws below stay inside these ranges and needn't reach their ends.
All inputs are finite; a program needn't handle non-finite values.
Results may differ from the reference program's by a relative error of at most 0.0055.
Values may be sent and summed in bfloat16 or wider, within the bound.
A program may use at most 128 MiB of HBM per device.

```python
import jax
import jax.numpy as jnp
from jax import lax

C = 512
WC = 32
FRAMES = 128
HH = 68


def levels(rng, dims, cuts, smallest, largest):
    factor_of = 1.0
    for position, blocks in cuts:
        draws = jax.random.uniform(jax.random.fold_in(jax.random.fold_in(rng, 6), position), (blocks,), jnp.float32, smallest / len(cuts), largest / len(cuts))
        factor_of = factor_of * jnp.repeat(jnp.exp(draws), dims[position] // blocks).reshape((-1,) + (1,) * (len(dims) - 1 - position))
    return factor_of


def noise(rng, dims, width, limit, shards=(), held_as=jnp.bfloat16):
    values = width * jax.random.normal(rng, dims, jnp.float32)
    if shards:
        values = values * levels(rng, dims, shards, -0.22, 0.18)
    return jnp.clip(values, -limit, limit).astype(held_as)


def setup_inputs(seed: int = 0) -> dict:
    splits = jax.random.split(jax.random.key(seed), 6)
    return {
        "video": noise(splits[0], (FRAMES, HH, WC, C), 1.0, 6.0, ((0, 32), (1, 2), (3, 4))),
        "depthwise_kernel": noise(splits[1], (3, 3, C), 9 ** -0.5, 2.0, ((2, 4),), jnp.float32),
        "down_weight": noise(splits[2], (3, C, C), (3 * C) ** -0.5, 0.15625, ((2, 4),)),
        "up_weight": noise(splits[3], (3, C, C), (2 * C) ** -0.5, 0.1875, ((2, 4),)),
        "cotangent": noise(splits[4], (FRAMES, HH, WC, C), 1.0, 6.0, ((0, 32), (1, 2), (3, 4))),
    }


def mix(frames, weight):
    shape = frames.shape
    flat = jnp.dot(frames.reshape(-1, shape[-1]), weight, preferred_element_type=jnp.float32)
    return flat.reshape(shape[:-1] + (weight.shape[1],))


def outer(left, right):
    return lax.dot_general(left.reshape(-1, left.shape[-1]), right.reshape(-1, right.shape[-1]), (((0,), (0,)), ((), ())), preferred_element_type=jnp.float32)


def bordered_image(field):
    return jnp.pad(field.astype(jnp.float32), ((0, 0), (1, 1), (1, 1), (0, 0)))


def reference(video, depthwise_kernel, down_weight, up_weight, cotangent):
    frames, row_count, column_count = video.shape[0], video.shape[1], video.shape[2]
    half = frames // 2
    vertical_padding = bordered_image(video)
    spatial_result = jnp.zeros(video.shape, jnp.float32)
    for first_operand in range(3):
        for second_operand in range(3):
            spatial_result = spatial_result + depthwise_kernel[first_operand, second_operand] * vertical_padding[:, first_operand:first_operand + row_count, second_operand:second_operand + column_count]
    spatial_result = spatial_result.astype(jnp.bfloat16)
    zero_two = jnp.zeros((2,) + video.shape[1:], jnp.bfloat16)
    spread = jnp.concatenate([zero_two, spatial_result], 0)
    sel0 = spread[2::2]
    sel1 = spread[1:frames + 1:2]
    sel2 = spread[0:frames:2]
    pre = mix(sel0, down_weight[0]) + mix(sel1, down_weight[1]) + mix(sel2, down_weight[2])
    latent = jax.nn.silu(pre).astype(jnp.bfloat16)
    latent_prev = jnp.concatenate([zero_two[:1], latent[:-1]], 0)
    even = mix(latent, up_weight[0]) + mix(latent_prev, up_weight[2])
    odd = mix(latent, up_weight[1])
    upper = jnp.stack([even, odd], 1).reshape(video.shape)
    result = (video.astype(jnp.float32) + upper).astype(jnp.bfloat16)
    g_even = cotangent[0::2]
    g_odd = cotangent[1::2]
    g_next = jnp.concatenate([cotangent, zero_two[:1]], 0)[2::2]
    grad_latent = mix(g_even, up_weight[0].T) + mix(g_odd, up_weight[1].T) + mix(g_next, up_weight[2].T)
    sig = jax.nn.sigmoid(pre)
    grad_pre = (grad_latent * sig * (1.0 + pre * (1.0 - sig))).astype(jnp.bfloat16)
    grad_after = jnp.concatenate([grad_pre, zero_two[:1]], 0)[1:]
    ga_even = mix(grad_pre, down_weight[0].T) + mix(grad_after, down_weight[2].T)
    ga_odd = mix(grad_after, down_weight[1].T)
    grad_spatial = jnp.stack([ga_even, ga_odd], 1).reshape(video.shape).astype(jnp.bfloat16)
    gpad = bordered_image(grad_spatial)
    back = cotangent.astype(jnp.float32)
    for first_operand in range(3):
        for second_operand in range(3):
            back = back + depthwise_kernel[first_operand, second_operand] * gpad[:, 2 - first_operand:2 - first_operand + row_count, 2 - second_operand:2 - second_operand + column_count]
    grad_video = back.astype(jnp.bfloat16)
    gradient_single32 = grad_spatial.astype(jnp.float32)
    depthwise_kernel_gradient = jnp.stack([jnp.stack([jnp.sum(vertical_padding[:, first_operand:first_operand + row_count, second_operand:second_operand + column_count] * gradient_single32, axis=(0, 1, 2)) for second_operand in range(3)], 0) for first_operand in range(3)], 0)
    grad_down = jnp.stack([outer(sel0, grad_pre), outer(sel1, grad_pre), outer(sel2, grad_pre)], 0)
    grad_up = jnp.stack([outer(latent, g_even), outer(latent, g_odd), outer(latent_prev, g_even)], 0)
    return result, grad_video, depthwise_kernel_gradient, grad_down, grad_up
```

```python
import jax
import jax.numpy as jnp
from jax import lax
from jax.sharding import PartitionSpec as P


def with_halo(value, sides, width):
    for axis, dim in sides:
        peers, length = (lax.axis_size(axis), value.shape[dim])
        up = [(i, (i + 1) % peers) for i in range(peers - 1)]
        down = [(j, i) for i, j in up]
        last = lax.slice_in_dim(value, length - width, length, axis=dim)
        first = lax.slice_in_dim(value, 0, width, axis=dim)
        before = lax.ppermute(last, axis, up)
        after = lax.ppermute(first, axis, down)
        value = jnp.concatenate([before, value, after], axis=dim)
    return value


def shifted(block, axis, distance):
    devices = range(lax.axis_size(axis))
    route = [(i - distance, i) for i in devices if i - distance in devices]
    return lax.ppermute(block, axis, route)


def mix(frames, weight):
    shape = frames.shape
    flat = jnp.dot(frames.reshape(-1, shape[-1]), weight, preferred_element_type=jnp.float32)
    return flat.reshape(shape[:-1] + (weight.shape[1],))


def outer(left, right):
    return lax.dot_general(
        left.reshape(-1, left.shape[-1]),
        right.reshape(-1, right.shape[-1]),
        (((0,), (0,)), ((), ())),
        preferred_element_type=jnp.float32,
    )


def stencil_apply(padded, kernel, row_count, column_count):
    total = jnp.zeros(padded.shape[:1] + (row_count, column_count) + padded.shape[3:], jnp.float32)
    for first_operand in range(3):
        for second_operand in range(3):
            total = (
                total
                + kernel[first_operand, second_operand]
                * padded[
                    :,
                    first_operand : first_operand + row_count,
                    second_operand : second_operand + column_count,
                ]
            )
    return total


def stencil_back(padded, kernel, start, row_count, column_count):
    total = start
    for first_operand in range(3):
        for second_operand in range(3):
            total = (
                total
                + kernel[first_operand, second_operand]
                * padded[
                    :,
                    2 - first_operand : 2 - first_operand + row_count,
                    2 - second_operand : 2 - second_operand + column_count,
                ]
            )
    return total


def depthwise_terms(vertical_padding, gradient_single32, row_count, column_count):
    return jnp.stack(
        [
            jnp.stack(
                [
                    jnp.sum(
                        vertical_padding[
                            :,
                            first_operand : first_operand + row_count,
                            second_operand : second_operand + column_count,
                        ]
                        * gradient_single32,
                        axis=(0, 1, 2),
                    )
                    for second_operand in range(3)
                ],
                0,
            )
            for first_operand in range(3)
        ],
        0,
    )


def shards(video, depthwise_kernel, down_weight, up_weight, cotangent):
    frames, row_count, column_count, shard = video.shape
    width = down_weight.shape[1]
    banded_matrix = with_halo(video, (("row", 1),), 1)
    vertical_padding = jnp.pad(banded_matrix.astype(jnp.float32), ((0, 0), (0, 0), (1, 1), (0, 0)))
    spatial_result = stencil_apply(
        vertical_padding, depthwise_kernel, row_count, column_count
    ).astype(jnp.bfloat16)
    spread = lax.all_gather(spatial_result, "chan", axis=3, tiled=True)
    even_frames = spread[0::2]
    odd_frames = spread[1::2]
    later = mix(odd_frames, down_weight[1]) + mix(even_frames, down_weight[2])
    carried = shifted(later[later.shape[0] - 1 :], "tm", 1)
    pre = mix(even_frames, down_weight[0]) + jnp.concatenate([carried, later[:-1]], 0)
    latent = jax.nn.silu(pre).astype(jnp.bfloat16)
    current = lax.all_gather(latent, "chan", axis=3, tiled=True)
    after = mix(current, up_weight[2])
    carried_up = shifted(after[after.shape[0] - 1 :], "tm", 1)
    even = mix(current, up_weight[0]) + jnp.concatenate([carried_up, after[:-1]], 0)
    odd = mix(current, up_weight[1])
    upper = jnp.stack([even, odd], 1).reshape(video.shape)
    result = (video.astype(jnp.float32) + upper).astype(jnp.bfloat16)
    g_first = shifted(cotangent[:1], "tm", -1)
    g_even = cotangent[0::2]
    g_odd = cotangent[1::2]
    g_next = jnp.concatenate([cotangent, g_first], 0)[2::2]
    latent_terms = (
        mix(g_even, up_weight[0].T) + mix(g_odd, up_weight[1].T) + mix(g_next, up_weight[2].T)
    )
    grad_latent = lax.psum_scatter(latent_terms.astype(jnp.bfloat16), "chan", scatter_dimension=3, tiled=True)
    sig = jax.nn.sigmoid(pre)
    grad_pre = (grad_latent * sig * (1.0 + pre * (1.0 - sig))).astype(jnp.bfloat16)
    pre_first = shifted(grad_pre[:1], "tm", -1)
    grad_ext = jnp.concatenate([grad_pre, pre_first], 0)
    ga_even = mix(grad_pre, down_weight[0].T) + mix(grad_ext[1:], down_weight[2].T)
    ga_odd = mix(grad_ext[1:], down_weight[1].T)
    terms = jnp.stack([ga_even, ga_odd], 1).reshape((frames, row_count, column_count, width))
    grad_spatial = lax.psum_scatter(terms.astype(jnp.bfloat16), "chan", scatter_dimension=3, tiled=True).astype(
        jnp.bfloat16
    )
    gband = with_halo(grad_spatial, (("row", 1),), 1)
    gpad = jnp.pad(gband.astype(jnp.float32), ((0, 0), (0, 0), (1, 1), (0, 0)))
    grad_video = stencil_back(
        gpad, depthwise_kernel, cotangent.astype(jnp.float32), row_count, column_count
    ).astype(jnp.bfloat16)
    gradient_single32 = grad_spatial.astype(jnp.float32)
    local_depthwise = depthwise_terms(vertical_padding, gradient_single32, row_count, column_count)
    following = grad_ext[1:]
    local = [
        local_depthwise.reshape(9, shard),
        jnp.zeros((7, shard), jnp.float32),
        outer(even_frames, grad_pre),
        outer(odd_frames, following),
        outer(even_frames, following),
        outer(current, g_even),
        outer(current, g_odd),
        outer(current, g_next),
    ]
    total = lax.psum(jnp.concatenate(local, 0), ("tm", "row"))
    channels = spread.shape[3]
    depthwise_kernel_gradient = total[:9].reshape(3, 3, shard)
    grad_down = total[16 : 16 + 3 * channels].reshape(3, channels, shard)
    grad_up = total[16 + 3 * channels :].reshape(3, channels, shard)
    return (result, grad_video, depthwise_kernel_gradient, grad_down, grad_up)


def solution(mesh):
    return jax.shard_map(
        shards,
        mesh=mesh,
        in_specs=(
            P("tm", "row", None, "chan"),
            P(None, None, "chan"),
            P(None, None, "chan"),
            P(None, None, "chan"),
            P("tm", "row", None, "chan"),
        ),
        out_specs=(
            P("tm", "row", None, "chan"),
            P("tm", "row", None, "chan"),
            P(None, None, "chan"),
            P(None, None, "chan"),
            P(None, None, "chan"),
        ),
        check_vma=False,
    )
```

```python
import functools

import jax
import jax.numpy as jnp
from jax import lax
from jax.experimental import pallas as pl
from jax.experimental.pallas import tpu as pltpu
from jax.sharding import PartitionSpec as P

MESH = pl.DeviceIdType.MESH
BF = jnp.bfloat16
F32 = jnp.float32

ROWS = 34
COLS = 32
PIXELS = ROWS * COLS
PART = PIXELS // 4
CH = 512
LANES = 128
EDGE = 8
WIDE = COLS + 2 * EDGE


def rem(a, n):
    return lax.rem(a, jnp.int32(n))


def div(a, n):
    return lax.div(a, jnp.int32(n))


def aligned(start, step, size):
    return pl.ds(pl.multiple_of(start, step), size)


def nn(a, b):
    return lax.dot_general(a, b, (((1,), (0,)), ((), ())), preferred_element_type=F32)


def nt(a, b):
    return lax.dot_general(a, b, (((1,), (1,)), ((), ())), preferred_element_type=F32)


def tn(a, b):
    return lax.dot_general(a, b, (((0,), (0,)), ((), ())), preferred_element_type=F32)


def body(
    video,
    dwk,
    down,
    up,
    cot,
    result,
    gvideo,
    gdepth,
    gdown,
    gup,
    vraw,
    craw,
    vpad,
    gpad,
    halo,
    ghalo,
    sp,
    s_all,
    g_all,
    w_all,
    pre,
    latent,
    upper,
    uchan,
    gpre,
    gspx,
    gs,
    resbuf,
    gvbuf,
    partial,
    core_out,
    core_in,
    xbuf,
    xin,
    zbuf,
    zin,
    ybuf,
    yin,
    total,
    dkx,
    dkp,
    dkz,
    dkout,
    ssem,
    rsem,
    lsem,
):
    t = lax.axis_index("tm")
    y = lax.axis_index("chan")
    row = lax.axis_index("row")
    core = rem(t, 2)
    xh = rem(div(t, 2), 2)
    z = div(t, 4)
    x = xh * 2 + row

    def at_x(xx, cc):
        return (z * 4 + div(xx, 2) * 2 + cc, y, rem(xx, 2))

    def at_z(zz):
        return (zz * 4 + xh * 2 + core, y, row)

    def at_y(yy):
        return (t, yy, row)

    def at_t(tt):
        return (tt, y, row)

    xs = [(d, rem(x + d, 4)) for d in (2, 1, 3)]
    ys = [(d, rem(y + d, 4)) for d in (2, 1, 3)]
    zs = [(d, rem(z + d, 8)) for d in (4, 3, 5, 2, 6, 1, 7)]
    partner = at_x(x, 1 - core)
    after = at_t(rem(t + 1, 32))
    before = at_t(rem(t + 31, 32))
    across = at_x(x + 1 - 2 * row, core)

    counts = [0, 0]
    started = []
    local = []

    def send(src, dst, device):
        i = counts[0]
        counts[0] += 1
        copy = pltpu.make_async_remote_copy(
            src_ref=src,
            dst_ref=dst,
            send_sem=ssem.at[i],
            recv_sem=rsem.at[i],
            device_id=device,
            device_id_type=MESH,
        )
        copy.start()
        started.append(copy)
        return copy

    def move(src, dst):
        i = counts[1]
        counts[1] += 1
        copy = pltpu.make_async_copy(src, dst, lsem.at[i])
        copy.start()
        return copy

    def arrive(copies):
        for copy in copies:
            copy.wait_recv()

    mine = aligned(y * PART, 8, PART)
    lanes = aligned(y * LANES, LANES, LANES)

    def chunk(j):
        return aligned(j * PART, 8, PART)

    video_in = move(video, vraw)
    cot_in = move(cot, craw)

    barrier = pltpu.get_barrier_semaphore()
    greet = [at_y(j) for _, j in ys] + [at_x(j, core) for _, j in xs] + [at_z(j) for _, j in zs] + [before, after]
    for device in greet:
        pl.semaphore_signal(barrier, inc=1, device_id=device, device_id_type=MESH)
    pl.semaphore_wait(barrier, len(greet))

    edge = (1 - row) * (ROWS - 1) * COLS
    halo_in = send(video.at[:, aligned(edge, 8, COLS), :], halo, across)

    wrow = core * 1536 + x * 384
    wmine = aligned(wrow, 8, 384)
    wsrc = aligned(x * 384, 8, 384)
    wbase = counts[0]
    counts[0] += 3
    wown = counts[1]
    counts[1] += 1

    def weight_copies(ref):
        found = [
            pltpu.make_async_remote_copy(
                src_ref=ref.at[wsrc, :],
                dst_ref=w_all.at[wmine, lanes],
                send_sem=ssem.at[wbase + n],
                recv_sem=rsem.at[wbase + n],
                device_id=at_y(j),
                device_id_type=MESH,
            )
            for n, (_, j) in enumerate(ys)
        ]
        return found, pltpu.make_async_copy(ref.at[wsrc, :], w_all.at[wmine, lanes], lsem.at[wown])

    @pl.when(core == 0)
    def _():
        found, own = weight_copies(down)
        for copy in found:
            copy.start()
        own.start()

    @pl.when(core == 1)
    def _():
        found, own = weight_copies(up)
        for copy in found:
            copy.start()
        own.start()

    w_in, w_own = weight_copies(down)
    started.extend(w_in)

    cot_a = [send(cot.at[0:2, chunk(j), :], g_all.at[0:2, :, lanes], at_y(j)) for _, j in ys]
    cot_own = move(cot.at[:, mine, :], g_all.at[0:4, :, lanes])

    taps = [dwk[j : j + 1, :] for j in range(9)]
    side = jnp.zeros((EDGE, LANES), F32)

    def clear(i, carry):
        for ref in (vpad, gpad):
            for f in range(4):
                ref[f, i, 0:EDGE, :] = side
                ref[f, i, EDGE + COLS : WIDE, :] = side
        return carry

    lax.fori_loop(0, ROWS + 2, clear, 0)
    video_in.wait()

    def fill(i, carry):
        for f in range(4):
            vpad[f, i + 1, EDGE : EDGE + COLS, :] = vraw[f, aligned(i * COLS, 8, COLS), :].astype(F32)
        return carry

    lax.fori_loop(0, ROWS, fill, 0)
    top = row == 1
    halo_in.wait_recv()
    for f in range(4):
        edge_row = halo[f, :, :].astype(F32)
        vpad[f, 0, EDGE : EDGE + COLS, :] = jnp.where(top, edge_row, 0.0)
        vpad[f, ROWS + 1, EDGE : EDGE + COLS, :] = jnp.where(top, 0.0, edge_row)

    def stencil(first):
        def run(i, carry):
            for f in (first, first + 1):
                acc = None
                for p in range(3):
                    for q in range(3):
                        term = taps[3 * p + q] * vpad[f, i + p, EDGE - 1 + q : EDGE - 1 + q + COLS, :]
                        acc = term if acc is None else acc + term
                sp[f, aligned(i * COLS, 8, COLS), :] = acc.astype(BF)
            return carry

        lax.fori_loop(0, ROWS, run, 0)

    stencil(2)
    sp_b = [send(sp.at[2:4, chunk(j), :], s_all.at[4:6, :, lanes], at_y(j)) for _, j in ys]
    sp_b_own = move(sp.at[2:4, mine, :], s_all.at[4:6, :, lanes])
    stencil(0)
    sp_a = [send(sp.at[0:2, chunk(j), :], s_all.at[2:4, :, lanes], at_y(j)) for _, j in ys]
    sp_a_own = move(sp.at[0:2, mine, :], s_all.at[2:4, :, lanes])
    cot_b = [send(cot.at[2:4, chunk(j), :], g_all.at[2:4, :, lanes], at_y(j)) for _, j in ys]

    arrive(w_in)
    w_own.wait()
    w_x = [send(w_all.at[wmine, :], w_all.at[wmine, :], at_x(j, core)) for _, j in xs]
    w_core = [send(w_all.at[wmine, :], w_all.at[wmine, :], partner)]

    arrive(cot_a)
    cot_own.wait()
    cot_next = send(g_all.at[0:1], g_all.at[4:5], before)
    arrive(sp_b)
    sp_b_own.wait()
    sp_prev = send(s_all.at[4:6], s_all.at[0:2], after)
    for (d, _), copy in zip(xs, w_x):
        copy.wait_recv()
        block = aligned(core * 1536 + rem(x + 4 - d, 4) * 384, 8, 384)
        w_core.append(send(w_all.at[block, :], w_all.at[block, :], partner))
    arrive(w_core)

    def wd(k):
        return w_all[k * CH : (k + 1) * CH, :]

    def wu(k):
        return w_all[3 * CH + k * CH : 3 * CH + (k + 1) * CH, :]

    def activate(m):
        value = nn(s_all[2 * m + 2], wd(0)) + nn(s_all[2 * m + 1], wd(1)) + nn(s_all[2 * m], wd(2))
        pre[m] = value
        latent[m + 1] = (value / (1.0 + jnp.exp(-value))).astype(BF)

    arrive(sp_a)
    sp_a_own.wait()
    activate(1)
    latent_prev = send(latent.at[2:3], latent.at[0:1], after)
    sp_prev.wait_recv()

    @pl.when(t == 0)
    def _():
        s_all[0:2] = jnp.zeros((2, PART, CH), BF)

    activate(0)
    upper[3] = nn(latent[2], wu(1)).astype(BF)
    upper[2] = (nn(latent[2], wu(0)) + nn(latent[1], wu(2))).astype(BF)
    up_b = [
        send(upper.at[2:4, :, aligned(j * LANES, LANES, LANES)], uchan.at[2:4, mine, :], at_y(j)) for _, j in ys
    ]
    up_b_own = move(upper.at[2:4, :, lanes], uchan.at[2:4, mine, :])
    upper[1] = nn(latent[1], wu(1)).astype(BF)
    latent_prev.wait_recv()

    @pl.when(t == 0)
    def _():
        latent[0] = jnp.zeros((PART, CH), BF)

    upper[0] = (nn(latent[1], wu(0)) + nn(latent[0], wu(2))).astype(BF)
    up_a = [
        send(upper.at[0:2, :, aligned(j * LANES, LANES, LANES)], uchan.at[0:2, mine, :], at_y(j)) for _, j in ys
    ]
    up_a_own = move(upper.at[0:2, :, lanes], uchan.at[0:2, mine, :])

    def backward(m):
        grad = nt(g_all[2 * m], wu(0)) + nt(g_all[2 * m + 1], wu(1)) + nt(g_all[2 * m + 2], wu(2))
        value = pre[m]
        sig = 1.0 / (1.0 + jnp.exp(-value))
        gpre[m] = (grad * sig * (1.0 + value * (1.0 - sig))).astype(BF)

    arrive(cot_b)
    backward(0)
    gpre_next = send(gpre.at[0:1], gpre.at[2:3], before)
    cot_next.wait_recv()
    last = t == 31

    @pl.when(last)
    def _():
        g_all[4] = jnp.zeros((PART, CH), BF)

    backward(1)
    gspx[0] = (nt(gpre[0], wd(0)) + nt(gpre[1], wd(2))).astype(BF)
    gspx[1] = nt(gpre[1], wd(1)).astype(BF)
    gs_a = [send(gspx.at[0:2, :, aligned(j * LANES, LANES, LANES)], gs.at[0:2, mine, :], at_y(j)) for _, j in ys]
    gs_a_own = move(gspx.at[0:2, :, lanes], gs.at[0:2, mine, :])

    partial[1536:2048, :] = tn(latent[1], g_all[0]) + tn(latent[2], g_all[2])
    partial[2048:2560, :] = tn(latent[1], g_all[1]) + tn(latent[2], g_all[3])
    partial[2560:3072, :] = tn(latent[1], g_all[2]) + tn(latent[2], g_all[4])
    gpre_next.wait_recv()

    @pl.when(last)
    def _():
        gpre[2] = jnp.zeros((PART, CH), BF)

    gspx[2] = (nt(gpre[1], wd(0)) + nt(gpre[2], wd(2))).astype(BF)
    gspx[3] = nt(gpre[2], wd(1)).astype(BF)
    gs_b = [send(gspx.at[2:4, :, aligned(j * LANES, LANES, LANES)], gs.at[2:4, mine, :], at_y(j)) for _, j in ys]
    gs_b_own = move(gspx.at[2:4, :, lanes], gs.at[2:4, mine, :])
    partial[0:512, :] = tn(s_all[2], gpre[0]) + tn(s_all[4], gpre[1])
    partial[512:1024, :] = tn(s_all[3], gpre[1]) + tn(s_all[5], gpre[2])
    partial[1024:1536, :] = tn(s_all[2], gpre[1]) + tn(s_all[4], gpre[2])

    def narrow(i, carry):
        core_out[aligned(i * 64, 64, 64), :] = partial[aligned((1 - core) * 1536 + i * 64, 64, 64), :].astype(BF)
        return carry

    lax.fori_loop(0, 24, narrow, 0)
    red_core = send(core_out, core_in, partner)

    def finish_result(first, copies, own):
        arrive(copies)
        own.wait()

        def run(i, carry):
            for f in (first, first + 1):
                part = aligned(i * COLS, 8, COLS)
                total_row = vraw[f, part, :].astype(F32) + uchan[f, part, :].astype(F32)
                resbuf[f, part, :] = total_row.astype(BF)
            return carry

        lax.fori_loop(0, ROWS, run, 0)
        local.append(move(resbuf.at[first : first + 2], result.at[first : first + 2]))

    finish_result(2, up_b, up_b_own)
    red_core.wait_recv()

    def widen(i, carry):
        part = aligned(i * 64, 64, 64)
        xbuf[part, :] = (partial[aligned(core * 1536 + i * 64, 64, 64), :] + core_in[part, :].astype(F32)).astype(BF)
        return carry

    lax.fori_loop(0, 24, widen, 0)
    red_x = [send(xbuf.at[aligned(j * 384, 8, 384), :], xin.at[d - 1], at_x(j, core)) for d, j in xs]
    finish_result(0, up_a, up_a_own)

    cot_in.wait()

    def gs_rows(first, copies, own):
        arrive(copies)
        own.wait()
        edges = send(
            gs.at[first : first + 2, aligned(edge, 8, COLS), :], ghalo.at[first : first + 2], across
        )

        def spread(i, carry):
            for f in (first, first + 1):
                gpad[f, i + 1, EDGE : EDGE + COLS, :] = gs[f, aligned(i * COLS, 8, COLS), :].astype(F32)
            return carry

        lax.fori_loop(0, ROWS, spread, 0)
        return edges

    def depth_terms(first, sums):
        def run(i, sums):
            sums = list(sums)
            for f in (first, first + 1):
                grad = gpad[f, i + 1, EDGE : EDGE + COLS, :]
                for p in range(3):
                    for q in range(3):
                        prod = vpad[f, i + p, EDGE - 1 + q : EDGE - 1 + q + COLS, :] * grad
                        n = 3 * p + q
                        sums[n] = sums[n] + ((prod[0:8] + prod[8:16]) + (prod[16:24] + prod[24:32]))
            return tuple(sums)

        return lax.fori_loop(0, ROWS, run, sums)

    def back(first, edges):
        edges.wait_recv()
        for f in (first, first + 1):
            edge_row = ghalo[f, :, :].astype(F32)
            gpad[f, 0, EDGE : EDGE + COLS, :] = jnp.where(top, edge_row, 0.0)
            gpad[f, ROWS + 1, EDGE : EDGE + COLS, :] = jnp.where(top, 0.0, edge_row)

        def run(i, carry):
            for f in (first, first + 1):
                part = aligned(i * COLS, 8, COLS)
                acc = craw[f, part, :].astype(F32)
                for p in range(3):
                    for q in range(3):
                        acc = acc + taps[3 * p + q] * gpad[f, i + 2 - p, EDGE + 1 - q : EDGE + 1 - q + COLS, :]
                gvbuf[f, part, :] = acc.astype(BF)
            return carry

        lax.fori_loop(0, ROWS, run, 0)
        local.append(move(gvbuf.at[first : first + 2], gvideo.at[first : first + 2]))

    edges_a = gs_rows(0, gs_a, gs_a_own)
    sums = depth_terms(0, tuple(jnp.zeros((8, LANES), F32) for _ in range(9)))
    back(0, edges_a)

    arrive(red_x)

    def sum_x(i, carry):
        part = aligned(i * 16, 16, 16)
        value = xbuf[aligned(x * 384 + i * 16, 16, 16), :].astype(F32)
        for n in range(3):
            value = value + xin[n, part, :].astype(F32)
        zbuf[part, :] = value.astype(BF)
        return carry

    lax.fori_loop(0, 24, sum_x, 0)
    red_z = [send(zbuf.at[aligned(j * 48, 8, 48), :], zin.at[d - 1], at_z(j)) for d, j in zs]

    edges_b = gs_rows(2, gs_b, gs_b_own)
    sums = depth_terms(2, sums)
    for n in range(9):
        dkout[n : n + 1, :] = jnp.sum(sums[n], axis=0, keepdims=True)
    dkout[9:16, :] = jnp.zeros((7, LANES), F32)
    dkx[x] = dkout[...]
    dk_x = [send(dkx.at[x], dkx.at[x], at_x(j, core)) for _, j in xs]
    arrive(red_z)
    value = zbuf[aligned(z * 48, 16, 48), :].astype(F32)
    for n in range(7):
        value = value + zin[n].astype(F32)
    ybuf[...] = value
    red_y = [send(ybuf.at[:, aligned(j * LANES, LANES, LANES)], yin.at[d - 1], at_y(j)) for d, j in ys]
    arrive(dk_x)
    dkp[0] = (dkx[0] + dkx[1]) + (dkx[2] + dkx[3])
    dk_core = send(dkp.at[0], dkp.at[1], partner)
    arrive(red_y)
    final = aligned(core * 1536 + x * 384 + z * 48, 8, 48)
    total[final, :] = (ybuf[:, lanes] + yin[0]) + (yin[1] + yin[2])
    gather_z = [send(total.at[final, :], total.at[final, :], at_z(j)) for _, j in zs]
    dk_core.wait_recv()
    dkz[z] = dkp[0] + dkp[1]
    dk_z = [send(dkz.at[z], dkz.at[z], at_z(j)) for _, j in zs]
    back(2, edges_b)
    arrive(gather_z)
    own_x = aligned(core * 1536 + x * 384, 8, 384)
    gather_x = [send(total.at[own_x, :], total.at[own_x, :], at_x(j, core)) for _, j in xs]
    gather_core = [send(total.at[own_x, :], total.at[own_x, :], partner)]
    arrive(dk_z)
    dk_sum = dkz[0]
    for n in range(1, 8):
        dk_sum = dk_sum + dkz[n]
    dkout[...] = dk_sum
    local.append(move(dkout, gdepth))
    for (d, _), copy in zip(xs, gather_x):
        copy.wait_recv()
        block = aligned(core * 1536 + rem(x + 4 - d, 4) * 384, 8, 384)
        gather_core.append(send(total.at[block, :], total.at[block, :], partner))
    arrive(gather_core)
    local.append(move(total.at[0:1536, :], gdown))
    local.append(move(total.at[1536:3072, :], gup))
    for copy in local:
        copy.wait()
    for copy in started:
        copy.wait_send()
    assert counts[0] <= SENDS and counts[1] <= MOVES, counts


SENDS = 80
MOVES = 20


def shards(video, depthwise_kernel, down_weight, up_weight, cotangent):
    frames = video.shape[0]
    flat = (frames, PIXELS, LANES)
    anywhere = pl.BlockSpec(memory_space=pl.ANY)
    inside = pl.BlockSpec(memory_space=pltpu.VMEM)
    vm = pltpu.VMEM
    taps = jnp.concatenate([depthwise_kernel.reshape(9, LANES), jnp.zeros((7, LANES), F32)], 0)
    outs = pl.pallas_call(
        body,
        out_shape=(
            jax.ShapeDtypeStruct(flat, BF),
            jax.ShapeDtypeStruct(flat, BF),
            jax.ShapeDtypeStruct((16, LANES), F32),
            jax.ShapeDtypeStruct((3 * CH, LANES), F32),
            jax.ShapeDtypeStruct((3 * CH, LANES), F32),
        ),
        in_specs=[anywhere, inside, anywhere, anywhere, anywhere],
        out_specs=(anywhere,) * 5,
        scratch_shapes=[
            vm(flat, BF),
            vm(flat, BF),
            vm((4, ROWS + 2, WIDE, LANES), F32),
            vm((4, ROWS + 2, WIDE, LANES), F32),
            vm((4, COLS, LANES), BF),
            vm((4, COLS, LANES), BF),
            vm(flat, BF),
            vm((6, PART, CH), BF),
            vm((5, PART, CH), BF),
            vm((6 * CH, CH), BF),
            vm((2, PART, CH), F32),
            vm((3, PART, CH), BF),
            vm((4, PART, CH), BF),
            vm(flat, BF),
            vm((3, PART, CH), BF),
            vm((4, PART, CH), BF),
            vm(flat, BF),
            vm(flat, BF),
            vm(flat, BF),
            vm((6 * CH, CH), F32),
            vm((3 * CH, CH), BF),
            vm((3 * CH, CH), BF),
            vm((3 * CH, CH), BF),
            vm((3, 384, CH), BF),
            vm((384, CH), BF),
            vm((7, 48, CH), BF),
            vm((48, CH), F32),
            vm((3, 48, LANES), F32),
            vm((6 * CH, LANES), F32),
            vm((4, 16, LANES), F32),
            vm((2, 16, LANES), F32),
            vm((8, 16, LANES), F32),
            vm((16, LANES), F32),
            pltpu.SemaphoreType.DMA((SENDS,)),
            pltpu.SemaphoreType.DMA((SENDS,)),
            pltpu.SemaphoreType.DMA((MOVES,)),
        ],
        compiler_params=pltpu.CompilerParams(
            collective_id=0, has_side_effects=True, vmem_limit_bytes=64 * 1024 * 1024 - 65536
        ),
    )(
        video.reshape(flat),
        taps,
        down_weight.reshape(3 * CH, LANES),
        up_weight.reshape(3 * CH, LANES),
        cotangent.reshape(flat),
    )
    res, gv, gd, gdw, guw = outs
    return (
        res.reshape(video.shape),
        gv.reshape(video.shape),
        gd[:9].reshape(3, 3, LANES),
        gdw.reshape(3, CH, LANES),
        guw.reshape(3, CH, LANES),
    )


def solution(mesh):
    return jax.shard_map(
        shards,
        mesh=mesh,
        in_specs=(
            P("tm", "row", None, "chan"),
            P(None, None, "chan"),
            P(None, None, "chan"),
            P(None, None, "chan"),
            P("tm", "row", None, "chan"),
        ),
        out_specs=(
            P("tm", "row", None, "chan"),
            P("tm", "row", None, "chan"),
            P(None, None, "chan"),
            P(None, None, "chan"),
            P(None, None, "chan"),
        ),
        check_vma=False,
    )
```

```python
import functools

import jax
import jax.numpy as jnp
from jax import lax
from jax.experimental import pallas as pl
from jax.experimental.pallas import tpu as pltpu
from jax.sharding import PartitionSpec as P

MESH = pl.DeviceIdType.MESH
BF = jnp.bfloat16
F32 = jnp.float32

ROWS = 34
COLS = 32
PIXELS = ROWS * COLS
PART = PIXELS // 4
CH = 512
LANES = 128
EDGE = 8
WIDE = COLS + 2 * EDGE


def rem(a, n):
    return lax.rem(a, jnp.int32(n))


def div(a, n):
    return lax.div(a, jnp.int32(n))


def aligned(start, step, size):
    return pl.ds(pl.multiple_of(start, step), size)


def slot(f):
    return f // 2 + 2 * (f % 2)


def nn(a, b):
    return lax.dot_general(a, b, (((1,), (0,)), ((), ())), preferred_element_type=F32)


def nt(a, b):
    return lax.dot_general(a, b, (((1,), (1,)), ((), ())), preferred_element_type=F32)


def tn(a, b):
    return lax.dot_general(a, b, (((0,), (0,)), ((), ())), preferred_element_type=F32)


def body(
    video,
    dwk,
    down,
    up,
    cot,
    result,
    gvideo,
    gdepth,
    gweights,
    vraw,
    craw,
    vpad,
    gpad,
    halo,
    ghalo,
    sp,
    s_all,
    g_all,
    w_all,
    pre,
    latent,
    upper,
    uchan,
    gpre,
    gspx,
    gs,
    resbuf,
    gvbuf,
    carry_out,
    carry_in,
    a_in,
    b_in,
    xbuf,
    xin,
    zbuf,
    zin,
    tbuf,
    tin,
    uin,
    ybuf,
    yin,
    total,
    dkx,
    dkp,
    dkz,
    ssem,
    rsem,
    lsem,
):
    t = lax.axis_index("tm")
    y = lax.axis_index("chan")
    row = lax.axis_index("row")
    core = rem(t, 2)
    xh = rem(div(t, 2), 2)
    z = div(t, 4)
    x = xh * 2 + row

    def at_x(xx, cc):
        return (z * 4 + div(xx, 2) * 2 + cc, y, rem(xx, 2))

    def at_z(zz):
        return (zz * 4 + xh * 2 + core, y, row)

    def at_y(yy):
        return (t, yy, row)

    def at_t(tt):
        return (tt, y, row)

    xs = [(d, rem(x + d, 4)) for d in (2, 1, 3)]
    ys = [(d, rem(y + d, 4)) for d in (2, 1, 3)]
    zs = [(d, rem(z + d, 8)) for d in (4, 3, 5, 2, 6, 1, 7)]
    partner = at_x(x, 1 - core)
    after = at_t(rem(t + 1, 32))
    before = at_t(rem(t + 31, 32))
    across = at_x(x + 1 - 2 * row, core)

    counts = [0, 0]
    started = []
    local = []

    def send(src, dst, device):
        i = counts[0]
        counts[0] += 1
        copy = pltpu.make_async_remote_copy(
            src_ref=src,
            dst_ref=dst,
            send_sem=ssem.at[i],
            recv_sem=rsem.at[i],
            device_id=device,
            device_id_type=MESH,
        )
        copy.start()
        started.append(copy)
        return copy

    def move(src, dst):
        i = counts[1]
        counts[1] += 1
        copy = pltpu.make_async_copy(src, dst, lsem.at[i])
        copy.start()
        return copy

    def arrive(copies):
        for copy in copies:
            copy.wait_recv()

    mine = aligned(y * PART, 8, PART)
    lanes = aligned(y * LANES, LANES, LANES)

    def chunk(j):
        return aligned(j * PART, 8, PART)


    def choose(first, second, device):
        i = counts[0]
        counts[0] += 1

        def make(src, dst):
            return pltpu.make_async_remote_copy(
                src_ref=src,
                dst_ref=dst,
                send_sem=ssem.at[i],
                recv_sem=rsem.at[i],
                device_id=device,
                device_id_type=MESH,
            )

        @pl.when(core == 0)
        def _():
            make(*first).start()

        @pl.when(core == 1)
        def _():
            make(*second).start()

        copy = make(*first)
        started.append(copy)
        return copy

    video_in = move(video, vraw)
    cot_in = move(cot, craw)

    barrier = pltpu.get_barrier_semaphore()
    greet = [at_y(j) for _, j in ys] + [at_x(j, core) for _, j in xs] + [at_z(j) for _, j in zs] + [before, after]
    for device in greet:
        pl.semaphore_signal(barrier, inc=1, device_id=device, device_id_type=MESH)

    side = jnp.zeros((EDGE, LANES), F32)

    def clear(i, carry):
        for ref in (vpad, gpad):
            for f in range(4):
                ref[f, i, 0:EDGE, :] = side
                ref[f, i, EDGE + COLS : WIDE, :] = side
        return carry

    lax.fori_loop(0, ROWS + 2, clear, 0)
    pl.semaphore_wait(barrier, len(greet))

    edge = (1 - row) * (ROWS - 1) * COLS
    halo_in = send(video.at[:, aligned(edge, 8, COLS), :], halo, across)

    wmine = aligned(core * 1536 + x * 384, 8, 384)
    wsrc = aligned(x * 384, 8, 384)
    w_in = [
        choose((down.at[wsrc, :], w_all.at[wmine, lanes]), (up.at[wsrc, :], w_all.at[wmine, lanes]), at_y(j))
        for _, j in ys
    ]
    wown = counts[1]
    counts[1] += 1

    @pl.when(core == 0)
    def _():
        pltpu.make_async_copy(down.at[wsrc, :], w_all.at[wmine, lanes], lsem.at[wown]).start()

    @pl.when(core == 1)
    def _():
        pltpu.make_async_copy(up.at[wsrc, :], w_all.at[wmine, lanes], lsem.at[wown]).start()

    w_own = pltpu.make_async_copy(down.at[wsrc, :], w_all.at[wmine, lanes], lsem.at[wown])

    def scatter(src, dst, frames):
        sent = [send(src.at[f, chunk(j), :], dst.at[slot(f), :, lanes], at_y(j)) for f in frames for _, j in ys]
        return sent, [move(src.at[f, mine, :], dst.at[slot(f), :, lanes]) for f in frames]

    def gather(src, dst, frames):
        sent = [
            send(src.at[f, :, aligned(j * LANES, LANES, LANES)], dst.at[f, mine, :], at_y(j))
            for f in frames
            for _, j in ys
        ]
        return sent, [move(src.at[f, :, lanes], dst.at[f, mine, :]) for f in frames]

    def landed(pair):
        arrive(pair[0])
        for copy in pair[1]:
            copy.wait()

    cot_0 = scatter(cot, g_all, (0,))
    cot_1 = scatter(cot, g_all, (1,))

    taps = [dwk[p, q : q + 1, :] for p in range(3) for q in range(3)]
    video_in.wait()

    def fill(i, carry):
        for f in range(4):
            vpad[f, i + 1, EDGE : EDGE + COLS, :] = vraw[f, aligned(i * COLS, 8, COLS), :].astype(F32)
        return carry

    lax.fori_loop(0, ROWS, fill, 0)
    top = row == 1
    halo_in.wait_recv()
    for f in range(4):
        edge_row = halo[f, :, :].astype(F32)
        vpad[f, 0, EDGE : EDGE + COLS, :] = jnp.where(top, edge_row, 0.0)
        vpad[f, ROWS + 1, EDGE : EDGE + COLS, :] = jnp.where(top, 0.0, edge_row)

    def stencil(first):
        def run(i, carry):
            for f in (first, first + 1):
                acc = None
                for p in range(3):
                    for q in range(3):
                        term = taps[3 * p + q] * vpad[f, i + p, EDGE - 1 + q : EDGE - 1 + q + COLS, :]
                        acc = term if acc is None else acc + term
                sp[f, aligned(i * COLS, 8, COLS), :] = acc.astype(BF)
            return carry

        lax.fori_loop(0, ROWS, run, 0)

    stencil(2)
    sp_b = scatter(sp, s_all, (2, 3))

    arrive(w_in)
    w_own.wait()
    w_x = [send(w_all.at[wmine, :], w_all.at[wmine, :], at_x(j, core)) for _, j in xs]
    w_core = [send(w_all.at[wmine, :], w_all.at[wmine, :], partner)]
    stencil(0)
    sp_a = scatter(sp, s_all, (0, 1))
    cot_b = scatter(cot, g_all, (2, 3))
    landed(cot_0)
    cot_next = send(g_all.at[0:1], g_all.at[4:5], before)
    for n in (1, 2, 0):
        w_x[n].wait_recv()
        block = aligned(core * 1536 + rem(x + 4 - xs[n][0], 4) * 384, 8, 384)
        w_core.append(send(w_all.at[block, :], w_all.at[block, :], partner))
    arrive(w_core)

    def wd(k):
        return w_all[k * CH : (k + 1) * CH, :]

    def wu(k):
        return w_all[3 * CH + k * CH : 3 * CH + (k + 1) * CH, :]

    def spatial(f):
        return s_all[slot(f)]

    def cotangent(f):
        return g_all[4 if f == 4 else slot(f)]

    def activate(m, value):
        pre[m] = value
        latent[m + 1] = (value / (1.0 + jnp.exp(-value))).astype(BF)

    landed(sp_b)
    carry_out[0] = (nn(spatial(3), wd(1)) + nn(spatial(2), wd(2))).astype(BF)
    carry = send(carry_out, carry_in, after)
    landed(sp_a)
    activate(1, nn(spatial(2), wd(0)) + nn(spatial(1), wd(1)) + nn(spatial(0), wd(2)))
    latent_prev = send(latent.at[2:3], latent.at[0:1], after)
    upper[3] = nn(latent[2], wu(1)).astype(BF)
    up_3 = gather(upper, uchan, (3,))
    first_value = nn(spatial(0), wd(0))
    carry.wait_recv()
    activate(0, first_value + jnp.where(t == 0, 0.0, carry_in[0].astype(F32)))
    upper[1] = nn(latent[1], wu(1)).astype(BF)
    up_1 = gather(upper, uchan, (1,))
    upper[2] = (nn(latent[2], wu(0)) + nn(latent[1], wu(2))).astype(BF)
    up_2 = gather(upper, uchan, (2,))

    def backward(m):
        grad = nt(cotangent(2 * m), wu(0)) + nt(cotangent(2 * m + 1), wu(1)) + nt(cotangent(2 * m + 2), wu(2))
        value = pre[m]
        sig = 1.0 / (1.0 + jnp.exp(-value))
        gpre[m] = (grad * sig * (1.0 + value * (1.0 - sig))).astype(BF)

    landed(cot_1)
    landed(cot_b)
    a_copy = choose((g_all.at[0:4], a_in), (s_all, a_in), partner)
    backward(0)
    gpre_next = send(gpre.at[0:1], gpre.at[2:3], before)
    cot_next.wait_recv()
    last = t == 31

    @pl.when(last)
    def _():
        g_all[4] = jnp.zeros((PART, CH), BF)

    backward(1)
    b_copy = choose((latent.at[1:3], b_in.at[1:3]), (gpre.at[0:2], b_in.at[0:2]), partner)
    gspx[0] = (nt(gpre[0], wd(0)) + nt(gpre[1], wd(2))).astype(BF)
    gspx[1] = nt(gpre[1], wd(1)).astype(BF)
    gs_a = gather(gspx, gs, (0, 1))
    latent_prev.wait_recv()

    @pl.when(t == 0)
    def _():
        latent[0] = jnp.zeros((PART, CH), BF)

    upper[0] = (nn(latent[1], wu(0)) + nn(latent[0], wu(2))).astype(BF)
    up_0 = gather(upper, uchan, (0,))

    def pair(ref, first):
        return ref[first : first + 2].reshape(2 * PART, CH)

    def weight_gradient(k):
        a = 2 * (k % 2)

        @pl.when(core == 0)
        def _():
            b = min(k, 1)
            xbuf[k] = (tn(pair(s_all, a), pair(gpre, b)) + tn(pair(a_in, a), pair(b_in, b))).astype(BF)

        @pl.when(core == 1)
        def _():
            b = 1 - k // 2
            xbuf[k] = (tn(pair(latent, b), pair(g_all, a)) + tn(pair(b_in, b), pair(a_in, a))).astype(BF)

    def to_x(k):
        return [send(xbuf.at[k, aligned(j * 128, 128, 128), :], xin.at[k, d - 1], at_x(j, core)) for d, j in xs]

    arrive([a_copy, b_copy])
    weight_gradient(0)
    red_x = to_x(0)
    gpre_next.wait_recv()

    @pl.when(last)
    def _():
        gpre[2] = jnp.zeros((PART, CH), BF)

    c_copy = choose((latent.at[0], b_in.at[0]), (gpre.at[2], b_in.at[2]), partner)
    gspx[2] = (nt(gpre[1], wd(0)) + nt(gpre[2], wd(2))).astype(BF)
    gspx[3] = nt(gpre[2], wd(1)).astype(BF)
    gs_b = gather(gspx, gs, (2, 3))
    arrive([c_copy])
    weight_gradient(1)
    red_x += to_x(1)
    weight_gradient(2)
    red_t = [send(xbuf.at[2, aligned(j * 64, 64, 64), :], tin.at[d - 1], at_z(j)) for d, j in zs]

    for frames in (up_3, up_1, up_2, up_0):
        landed(frames)

    def add_up(i, carry):
        for f in range(4):
            part = aligned(i * COLS, 8, COLS)
            resbuf[f, part, :] = (vraw[f, part, :].astype(F32) + uchan[f, part, :].astype(F32)).astype(BF)
        return carry

    lax.fori_loop(0, ROWS, add_up, 0)
    local.append(move(resbuf, result))

    cot_in.wait()

    def gs_rows(first, frames):
        landed(frames)
        edges = send(gs.at[first : first + 2, aligned(edge, 8, COLS), :], ghalo.at[first : first + 2], across)

        def spread(i, carry):
            for f in (first, first + 1):
                gpad[f, i + 1, EDGE : EDGE + COLS, :] = gs[f, aligned(i * COLS, 8, COLS), :].astype(F32)
            return carry

        lax.fori_loop(0, ROWS, spread, 0)
        return edges

    def depth_terms(first, sums):
        def run(i, sums):
            sums = list(sums)
            for f in (first, first + 1):
                grad = gpad[f, i + 1, EDGE : EDGE + COLS, :]
                for p in range(3):
                    for q in range(3):
                        prod = vpad[f, i + p, EDGE - 1 + q : EDGE - 1 + q + COLS, :] * grad
                        n = 3 * p + q
                        sums[n] = sums[n] + ((prod[0:8] + prod[8:16]) + (prod[16:24] + prod[24:32]))
            return tuple(sums)

        return lax.fori_loop(0, ROWS, run, sums)

    def back(first, edges):
        edges.wait_recv()
        for f in (first, first + 1):
            edge_row = ghalo[f, :, :].astype(F32)
            gpad[f, 0, EDGE : EDGE + COLS, :] = jnp.where(top, edge_row, 0.0)
            gpad[f, ROWS + 1, EDGE : EDGE + COLS, :] = jnp.where(top, 0.0, edge_row)

        def run(i, carry):
            for f in (first, first + 1):
                part = aligned(i * COLS, 8, COLS)
                acc = craw[f, part, :].astype(F32)
                for p in range(3):
                    for q in range(3):
                        acc = acc + taps[3 * p + q] * gpad[f, i + 2 - p, EDGE + 1 - q : EDGE + 1 - q + COLS, :]
                gvbuf[f, part, :] = acc.astype(BF)
            return carry

        lax.fori_loop(0, ROWS, run, 0)
        local.append(move(gvbuf.at[first : first + 2], gvideo.at[first : first + 2]))

    edges_a = gs_rows(0, gs_a)
    sums = depth_terms(0, tuple(jnp.zeros((8, LANES), F32) for _ in range(9)))

    arrive(red_x)
    for k in range(2):

        def sum_x(i, carry):
            part = aligned(i * 16, 16, 16)
            value = xbuf[k, aligned(x * 128 + i * 16, 16, 16), :].astype(F32)
            for n in range(3):
                value = value + xin[k, n, part, :].astype(F32)
            zbuf[k, part, :] = value.astype(BF)
            return carry

        lax.fori_loop(0, 8, sum_x, 0)
    red_z = [send(zbuf.at[:, aligned(j * 16, 16, 16), :], zin.at[d - 1], at_z(j)) for d, j in zs]
    back(0, edges_a)
    arrive(red_t)

    def sum_t(i, carry):
        part = aligned(i * 16, 16, 16)
        value = xbuf[2, aligned(z * 64 + i * 16, 16, 16), :].astype(F32)
        for n in range(7):
            value = value + tin[n, part, :].astype(F32)
        tbuf[part, :] = value.astype(BF)
        return carry

    lax.fori_loop(0, 4, sum_t, 0)
    red_u = [send(tbuf.at[aligned(j * 16, 16, 16), :], uin.at[d - 1], at_x(j, core)) for d, j in xs]

    edges_b = gs_rows(2, gs_b)
    sums = depth_terms(2, sums)
    dkx[x] = jnp.zeros((16, LANES), F32)
    for n in range(9):
        dkx[x, n : n + 1, :] = jnp.sum(sums[n], axis=0, keepdims=True)
    dk_x = [send(dkx.at[x], dkx.at[x], at_x(j, core)) for _, j in xs]

    arrive(red_z)
    for k in range(2):
        value = zbuf[k, aligned(z * 16, 16, 16), :].astype(F32)
        for n in range(7):
            value = value + zin[n, k].astype(F32)
        ybuf[16 * k : 16 * k + 16, :] = value
    arrive(red_u)
    value = tbuf[aligned(x * 16, 16, 16), :].astype(F32)
    for n in range(3):
        value = value + uin[n].astype(F32)
    ybuf[32:48, :] = value
    red_y = [send(ybuf.at[:, aligned(j * LANES, LANES, LANES)], yin.at[d - 1], at_y(j)) for d, j in ys]
    arrive(dk_x)
    dkp[0] = (dkx[0] + dkx[1]) + (dkx[2] + dkx[3])
    dk_core = send(dkp.at[0], dkp.at[1], partner)
    arrive(red_y)
    final = ((ybuf[:, lanes] + yin[0]) + (yin[1] + yin[2])).astype(BF)
    fine = aligned(x * 128 + z * 16, 16, 16)
    total[core, 0, fine, :] = final[0:16]
    total[core, 1, fine, :] = final[16:32]
    thin = aligned(z * 64 + x * 16, 16, 16)
    total[core, 2, thin, :] = final[32:48]
    own = total.at[core]
    gather_z = [send(own.at[0:2, fine, :], own.at[0:2, fine, :], at_z(j)) for _, j in zs]
    gather_u = [send(own.at[2, thin, :], own.at[2, thin, :], at_x(j, core)) for _, j in xs]
    dk_core.wait_recv()
    dkz[z] = dkp[0] + dkp[1]
    dk_z = [send(dkz.at[z], dkz.at[z], at_z(j)) for _, j in zs]
    back(2, edges_b)
    arrive(gather_u)
    broad = aligned(z * 64, 64, 64)
    gather_t = [send(own.at[2, broad, :], own.at[2, broad, :], at_z(j)) for _, j in zs]
    arrive(gather_z)

    def block(xx):
        return aligned(xx * 128, 128, 128)

    gather_x = [send(own.at[0:2, block(x), :], own.at[0:2, block(x), :], at_x(j, core)) for _, j in xs]
    ends = [send(own.at[0:2, block(x), :], own.at[0:2, block(x), :], partner)]
    arrive(dk_z)
    dk_sum = dkz[0]
    for n in range(1, 8):
        dk_sum = dk_sum + dkz[n]
    for p in range(3):
        gdepth[p] = dk_sum[3 * p : 3 * p + 3, :]
    for (d, _), copy in zip(xs, gather_x):
        copy.wait_recv()
        there = block(rem(x + 4 - d, 4))
        ends.append(send(own.at[0:2, there, :], own.at[0:2, there, :], partner))
    arrive(gather_t)
    ends.append(send(own.at[2], own.at[2], partner))
    arrive(ends)
    local.append(move(total, gweights))
    for copy in local:
        copy.wait()
    for copy in started:
        copy.wait_send()
    assert counts[0] <= SENDS and counts[1] <= MOVES, counts


SENDS = 152
MOVES = 24


def shards(video, depthwise_kernel, down_weight, up_weight, cotangent):
    frames = video.shape[0]
    flat = (frames, PIXELS, LANES)
    anywhere = pl.BlockSpec(memory_space=pl.ANY)
    inside = pl.BlockSpec(memory_space=pltpu.VMEM)
    vm = pltpu.VMEM
    res, gv, gd, gw = pl.pallas_call(
        body,
        out_shape=(
            jax.ShapeDtypeStruct(flat, BF),
            jax.ShapeDtypeStruct(flat, BF),
            jax.ShapeDtypeStruct((3, 3, LANES), F32),
            jax.ShapeDtypeStruct((2, 3, CH, LANES), BF),
        ),
        in_specs=[anywhere, inside, anywhere, anywhere, anywhere],
        out_specs=(anywhere, anywhere, inside, anywhere),
        scratch_shapes=[
            vm(flat, BF),
            vm(flat, BF),
            vm((4, ROWS + 2, WIDE, LANES), F32),
            vm((4, ROWS + 2, WIDE, LANES), F32),
            vm((4, COLS, LANES), BF),
            vm((4, COLS, LANES), BF),
            vm(flat, BF),
            vm((4, PART, CH), BF),
            vm((5, PART, CH), BF),
            vm((6 * CH, CH), BF),
            vm((2, PART, CH), F32),
            vm((3, PART, CH), BF),
            vm((4, PART, CH), BF),
            vm(flat, BF),
            vm((3, PART, CH), BF),
            vm((4, PART, CH), BF),
            vm(flat, BF),
            vm(flat, BF),
            vm(flat, BF),
            vm((1, PART, CH), BF),
            vm((1, PART, CH), BF),
            vm((4, PART, CH), BF),
            vm((3, PART, CH), BF),
            vm((3, CH, CH), BF),
            vm((2, 3, 128, CH), BF),
            vm((2, 128, CH), BF),
            vm((7, 2, 16, CH), BF),
            vm((64, CH), BF),
            vm((7, 64, CH), BF),
            vm((3, 16, CH), BF),
            vm((48, CH), F32),
            vm((3, 48, LANES), F32),
            vm((2, 3, CH, LANES), BF),
            vm((4, 16, LANES), F32),
            vm((2, 16, LANES), F32),
            vm((8, 16, LANES), F32),
            pltpu.SemaphoreType.DMA((SENDS,)),
            pltpu.SemaphoreType.DMA((SENDS,)),
            pltpu.SemaphoreType.DMA((MOVES,)),
        ],
        compiler_params=pltpu.CompilerParams(
            collective_id=0, has_side_effects=True, vmem_limit_bytes=64 * 1024 * 1024 - 65536
        ),
    )(
        video.reshape(flat),
        depthwise_kernel,
        down_weight.reshape(3 * CH, LANES),
        up_weight.reshape(3 * CH, LANES),
        cotangent.reshape(flat),
    )
    gw = gw.astype(F32)
    return res.reshape(video.shape), gv.reshape(video.shape), gd, gw[0], gw[1]


def solution(mesh):
    return jax.shard_map(
        shards,
        mesh=mesh,
        in_specs=(
            P("tm", "row", None, "chan"),
            P(None, None, "chan"),
            P(None, None, "chan"),
            P(None, None, "chan"),
            P("tm", "row", None, "chan"),
        ),
        out_specs=(
            P("tm", "row", None, "chan"),
            P("tm", "row", None, "chan"),
            P(None, None, "chan"),
            P(None, None, "chan"),
            P(None, None, "chan"),
        ),
        check_vma=False,
    )
```
